32 devices in a mesh: grp: 2 (over y), blk: 4 (over z), walk: 2 (over x), sub: 2 (over core).
Axes of the slice: x: 2, y: 2, z: 4, core: 2. Of those that a mesh axis runs over, the one named last changes fastest.
Arguments:
- walker_mats: bfloat16 [8, 2048, 2048], P(('grp', 'blk'), 'walk'), parts along dimension 0, may hold values from -0.0029296875 to 0.0029296875
- vertex: int32 [8, 2048], P(('grp', 'blk')), parts along dimension 0, may hold values from 0 to 8191
- weights: float32 [8], P('grp'), parts along dimension 0, may hold values from 0.5 to 1.5
- transfer_table: int32 [16, 2560], replicated, may hold values from 0 to 2559, each once within a row
- g4_old: float32 [32, 16, 2560], P(('grp', 'blk', 'walk', 'sub')), parts along dimension 0, may hold values from -2 to 2
Outputs:
- g4_new: float32 [32, 16, 2560], P(('grp', 'blk', 'walk', 'sub')), parts along dimension 0
The draws below stay inside these ranges and needn't reach their ends.
There are 2 independent parts, one for each index of `grp`. The reference program is written for one: setup_inputs(seed, part) draws one part's arguments, and reference() takes and returns one part's arrays. A program takes and returns all parts, laid end to end along the dimension named above; an argument that names none is the same for every part. Nothing has to cross between parts.
All inputs are finite; a program needn't handle non-finite values.
Results may differ from the reference program's by a relative error of at most 0.0041.
Values may be sent and summed in bfloat16 or wider, within the bound.
A program may use at most 64 MiB of HBM per device.

```python
import math
import jax
import jax.numpy as jnp
from jax import lax

NV = 2048
K2 = 2560
TQ = 4
RSTEPS = 4
NW = 4
K1 = 16
NQ = 16
STRIDE = 4


def place_ends(drawn, stream_key, smallest, top_value):
    longest = drawn.shape.index(max(drawn.shape))
    spots = []
    for shift in (0, 1):
        where = [jax.random.randint(jax.random.fold_in(stream_key, axis), (), 0, length) for axis, length in enumerate(drawn.shape)]
        where[longest] = (where[longest] + shift) % drawn.shape[longest]
        spots.append(tuple(where))
    return drawn.at[spots[0]].set(smallest).at[spots[1]].set(top_value)


def block_scale(key, dims, cuts, least, high):
    level, own = 1.0, jax.random.fold_in(key, 6)
    for dim, parts in cuts:
        steps = jnp.exp(jax.random.uniform(jax.random.fold_in(own, dim), (parts,), jnp.float32, least / len(cuts), high / len(cuts)))
        level = level * jnp.repeat(steps, dims[dim] // parts).reshape([-1 if axis == dim else 1 for axis in range(len(dims))])
    return level


def noise(stream_key, dims, spread, most, cuts=(), held_as=jnp.bfloat16):
    drawn = spread * jax.random.normal(stream_key, dims, jnp.float32)
    if cuts:
        drawn = drawn * block_scale(stream_key, dims, cuts, -0.22, 0.18)
    return jnp.clip(drawn, -most, most).astype(held_as)


def setup_inputs(seed: int = 0, part: int = 0) -> dict:
    key_of = jax.random.split(jax.random.key(seed), 6)
    own_keys = jax.random.split(jax.random.fold_in(key_of[5], part), 6)
    return {
        "walker_mats": noise(own_keys[0], (NW, NV, NV), (NV * NV) ** -0.5, 0.0029296875, ((0, 4), (1, 2))),
        "vertex": place_ends(jax.random.randint(own_keys[1], (NW, NV), 0, 8192), jax.random.fold_in(own_keys[1], 1), 0, 8191).astype(jnp.int32),
        "weights": jnp.clip(jax.random.uniform(own_keys[2], (NW,), jnp.float32, 0.5, 1.5), 0.5, 1.5),
        "transfer_table": jax.vmap(lambda own: jax.random.permutation(own, K2))(jax.random.split(key_of[3], NQ)).reshape((NQ, K2)).astype(jnp.int32),
        "g4_old": noise(own_keys[4], (K1, NQ, K2), 0.3, 2.0, ((0, 16),), jnp.float32),
    }


phase_period = 8192


def cas_table(vertices, frequencies):
    residue = (vertices[:, None] * frequencies[None, :]) % phase_period
    angles = residue.astype(jnp.float32) * (2.0 * math.pi / phase_period)
    return (jnp.cos(angles) + jnp.sin(angles)).astype(jnp.bfloat16)


def reference(walker_mats, vertex, weights, transfer_table, g4_old):
    frequencies = jnp.arange(K2, dtype=jnp.int32)

    def transform_walker(walker_item):
        matrix, vertices = walker_item
        cas_rows = cas_table(vertices, frequencies)
        half_transform = jnp.dot(matrix, cas_rows, preferred_element_type=jnp.float32).astype(jnp.bfloat16)
        return jnp.dot(cas_rows[:, :K1].T, half_transform, preferred_element_type=jnp.float32).astype(jnp.bfloat16)

    greens = lax.map(transform_walker, (walker_mats, vertex))
    scaled = greens.astype(jnp.float32) * (weights / NW)[:, None, None]
    panels = []
    for cycle_step in range(RSTEPS):
        shifted = jnp.roll(greens, cycle_step * STRIDE, axis=1)
        for transfer in range(TQ):
            picked = jnp.take(shifted, transfer_table[cycle_step * TQ + transfer], axis=2).astype(jnp.float32)
            panels.append(jnp.sum(scaled * picked, axis=0))
    return g4_old + jnp.stack(panels, axis=1)
```

```python
import functools
import math

import jax
import jax.numpy as jnp
import numpy as np
from jax import lax
from jax.experimental import pallas as pl
from jax.experimental.pallas import tpu as pltpu
from jax.sharding import PartitionSpec as P

TQ = 4
RSTEPS = 4

phase_period = 8192
quarter = phase_period // 4
lanes = 128
fine_count = 64
column_block = 256


def cos_sin(residue):
    turns = (residue + quarter // 2) >> 11
    x = (residue - (turns << 11)).astype(jnp.float32) * (2.0 * math.pi / phase_period)
    y = x * x
    s = x + x * y * (-1 / 6 + y * (1 / 120 + y * (-1 / 5040 + y * (1 / 362880))))
    c = 1.0 + y * (-0.5 + y * (1 / 24 + y * (-1 / 720 + y * (1 / 40320 + y * (-1 / 3628800)))))
    odd = (turns & 1) == 1
    cos = jnp.where(odd, s, c)
    sin = jnp.where(odd, c, s)
    cos = jnp.where(((turns + 1) & 2) == 2, -cos, cos)
    sin = jnp.where((turns & 2) == 2, -sin, sin)
    return cos, sin


def green_kernel(
    mats, vertex, window, gathered,
    slab, fine_plus, fine_minus, coarse_cos, coarse_sin, pair, partial, landed, mine,
    slab_sem, send_one, recv_one, send_two, recv_two,
):
    blk_count, walk_count, sub_count = (lax.axis_size(a) for a in ("blk", "walk", "sub"))
    b, w, s = (lax.axis_index(a) for a in ("blk", "walk", "sub"))
    near = walk_count * sub_count
    place = w * sub_count + s
    depth = slab.shape[1]
    own_rows = slab.shape[0]
    start = pl.multiple_of(s * depth, lanes)
    fetch = pltpu.make_async_copy(mats.at[0, :, pl.ds(start, depth)], slab, slab_sem)
    fetch.start()

    def near_id(distance):
        peer = lax.rem(place + distance, near)
        return {"walk": peer // sub_count, "sub": lax.rem(peer, sub_count)}

    def far_id(distance):
        return {"blk": lax.rem(b + distance, blk_count)}

    barrier = pltpu.get_barrier_semaphore()
    for d in range(1, near):
        pl.semaphore_signal(barrier, inc=1, device_id=near_id(d), device_id_type=pl.DeviceIdType.MESH)
    for d in range(1, blk_count):
        pl.semaphore_signal(barrier, inc=1, device_id=far_id(d), device_id_type=pl.DeviceIdType.MESH)

    verts = vertex[:, pl.ds(start, depth)]
    fine = lax.broadcasted_iota(jnp.int32, (fine_count, depth), 0)
    cos, sin = cos_sin((fine * verts) & (phase_period - 1))
    fine_plus[...] = cos + sin
    fine_minus[...] = cos - sin
    coarse = lax.broadcasted_iota(jnp.int32, coarse_cos.shape, 0) * fine_count
    cos, sin = cos_sin((coarse * verts) & (phase_period - 1))
    coarse_cos[...] = cos
    coarse_sin[...] = sin
    own = vertex[:, pl.ds(pl.multiple_of(w * own_rows, lanes), own_rows)]
    cos, sin = cos_sin((window[...] * own) & (phase_period - 1))
    left = (cos + sin).astype(jnp.bfloat16)

    fetch.wait()
    inner = jnp.dot(left, slab[...], preferred_element_type=jnp.float32)
    rows = inner.shape[0]
    high = inner.astype(jnp.bfloat16)
    pair[0:rows, :] = high
    pair[rows:2 * rows, :] = (inner - high.astype(jnp.float32)).astype(jnp.bfloat16)

    per_block = column_block // fine_count
    share = rows // near

    @pl.loop(0, partial.shape[2] // column_block)
    def _(block):
        pieces = []
        for part in range(per_block):
            row = block * per_block + part
            c = coarse_cos[pl.ds(row, 1), :]
            t = coarse_sin[pl.ds(row, 1), :]
            pieces.append((c * fine_plus[...] + t * fine_minus[...]).astype(jnp.bfloat16))
        table = jnp.concatenate(pieces, axis=0)
        both = lax.dot_general(
            pair[...], table, (((1,), (1,)), ((), ())), preferred_element_type=jnp.float32
        )
        total = both[0:rows] + both[rows:2 * rows]
        columns = pl.ds(pl.multiple_of(block * column_block, column_block), column_block)
        for q in range(near):
            partial[q, :, columns] = total[q * share:(q + 1) * share]

    pl.semaphore_wait(barrier, near - 1 + blk_count - 1)
    first = []
    for d in range(1, near):
        copy = pltpu.make_async_remote_copy(
            src_ref=partial.at[lax.rem(place + d, near)],
            dst_ref=landed.at[d - 1],
            send_sem=send_one.at[d - 1],
            recv_sem=recv_one.at[d - 1],
            device_id=near_id(d),
            device_id_type=pl.DeviceIdType.MESH,
        )
        copy.start()
        first.append(copy)
    total = partial[place]
    for d in range(1, near):
        first[d - 1].wait_recv()
        total = total + landed[d - 1]
    mine[...] = total.astype(jnp.bfloat16)
    gathered[b] = total.astype(jnp.bfloat16)
    second = []
    for d in range(1, blk_count):
        copy = pltpu.make_async_remote_copy(
            src_ref=mine,
            dst_ref=gathered.at[b],
            send_sem=send_two.at[d - 1],
            recv_sem=recv_two.at[d - 1],
            device_id=far_id(d),
            device_id_type=pl.DeviceIdType.MESH,
        )
        copy.start()
        second.append(copy)
    for copy in first:
        copy.wait_send()
    for copy in second:
        copy.wait()


def panel_kernel(weights, gathered, table, old, new, wide, source, scaled):
    walkers, rows, columns = gathered.shape
    blk_count = lax.axis_size("blk")
    rows_own = rows // blk_count
    b = lax.axis_index("blk")
    transfers = table.shape[0]
    sublanes = 8
    blocks = columns // lanes
    for n in range(walkers):
        wide[n] = gathered[n].astype(jnp.float32)
    for inner in range(rows_own):
        for n in range(walkers):
            for step in range(RSTEPS):
                row = lax.rem(b + RSTEPS * blk_count - step, blk_count) * rows_own + inner
                line = wide[n, pl.ds(row, 1), :]
                source[n, step * TQ:(step + 1) * TQ, :] = jnp.broadcast_to(line, (TQ, columns))
                if step == 0:
                    scaled[n, :, :] = jnp.broadcast_to(line * (weights[n] / walkers), (sublanes, columns))

        @pl.loop(0, blocks)
        def _(block):
            here = pl.ds(pl.multiple_of(block * lanes, lanes), lanes)
            for half in range(transfers // sublanes):
                span = slice(half * sublanes, (half + 1) * sublanes)
                index = table[span, here]
                low = index & (lanes - 1)
                which = index >> 7
                picked = [jnp.zeros((sublanes, lanes), jnp.float32) for _ in range(walkers)]
                for k in range(blocks):
                    hit = which == k
                    for n in range(walkers):
                        found = jnp.take_along_axis(
                            source[n, span, k * lanes:(k + 1) * lanes], low, axis=1,
                            mode="promise_in_bounds",
                        )
                        picked[n] = jnp.where(hit, found, picked[n])
                total = picked[0] * scaled[0, :, here]
                for n in range(1, walkers):
                    total = total + picked[n] * scaled[n, :, here]
                new[inner, span, here] = old[inner, span, here] + total


def local(walker_mats, vertex, weights, transfer_table, g4_old):
    blk_count, walk_count, sub_count = (lax.axis_size(a) for a in ("blk", "walk", "sub"))
    near = walk_count * sub_count
    rows_own, transfers, columns = g4_old.shape
    own_rows, vertices = walker_mats.shape[1:]
    depth = vertices // sub_count
    share = blk_count * rows_own
    rows = near * share
    p = np.arange(rows)
    inner, blk_part, near_part = p % rows_own, p // rows_own % blk_count, p // share
    window = jnp.asarray(((blk_part * near + near_part) * rows_own + inner)[:, None], jnp.int32)
    vmem = pl.BlockSpec(memory_space=pltpu.VMEM)
    gathered = pl.pallas_call(
        green_kernel,
        out_shape=jax.ShapeDtypeStruct((blk_count, share, columns), jnp.bfloat16),
        in_specs=[pl.BlockSpec(memory_space=pl.ANY), vmem, vmem],
        out_specs=vmem,
        scratch_shapes=[
            pltpu.VMEM((own_rows, depth), jnp.bfloat16),
            pltpu.VMEM((fine_count, depth), jnp.float32),
            pltpu.VMEM((fine_count, depth), jnp.float32),
            pltpu.VMEM((columns // fine_count, depth), jnp.float32),
            pltpu.VMEM((columns // fine_count, depth), jnp.float32),
            pltpu.VMEM((2 * rows, depth), jnp.bfloat16),
            pltpu.VMEM((near, share, columns), jnp.float32),
            pltpu.VMEM((near - 1, share, columns), jnp.float32),
            pltpu.VMEM((share, columns), jnp.bfloat16),
            pltpu.SemaphoreType.DMA,
            pltpu.SemaphoreType.DMA((near - 1,)),
            pltpu.SemaphoreType.DMA((near - 1,)),
            pltpu.SemaphoreType.DMA((blk_count - 1,)),
            pltpu.SemaphoreType.DMA((blk_count - 1,)),
        ],
        compiler_params=pltpu.CompilerParams(collective_id=0, has_side_effects=True),
        name="green",
    )(walker_mats, vertex, window)
    return pl.pallas_call(
        panel_kernel,
        out_shape=jax.ShapeDtypeStruct(g4_old.shape, jnp.float32),
        in_specs=[pl.BlockSpec(memory_space=pltpu.SMEM), vmem, vmem, vmem],
        out_specs=vmem,
        scratch_shapes=[
            pltpu.VMEM((blk_count, share, columns), jnp.float32),
            pltpu.VMEM((blk_count, transfers, columns), jnp.float32),
            pltpu.VMEM((blk_count, 8, columns), jnp.float32),
        ],
        name="panels",
    )(weights, gathered, transfer_table, g4_old)


def solution(mesh):
    in_specs = (
        P(("grp", "blk"), "walk", None),
        P(("grp", "blk"), None),
        P("grp"),
        P(),
        P(("grp", "blk", "walk", "sub"), None, None),
    )
    out_specs = P(("grp", "blk", "walk", "sub"), None, None)
    return jax.shard_map(local, mesh=mesh, in_specs=in_specs, out_specs=out_specs, check_vma=False)
```

```python
import math

import jax
import jax.numpy as jnp
import numpy as np
from jax import lax
from jax.experimental import pallas as pl
from jax.experimental.pallas import tpu as pltpu
from jax.sharding import PartitionSpec as P

TQ = 4
RSTEPS = 4

half_period = 16384
lanes = 128
sublanes = 8
column_block = 256
chunk_blocks = 2
group_blocks = 4


def cos_sin(residue):
    turns = (residue + half_period // 8) >> 12
    x = (residue - (turns << 12)).astype(jnp.float32) * (2.0 * math.pi / half_period)
    y = x * x
    s = x + x * y * (-1 / 6 + y * (1 / 120 + y * (-1 / 5040 + y * (1 / 362880))))
    c = 1.0 + y * (-0.5 + y * (1 / 24 + y * (-1 / 720 + y * (1 / 40320 + y * (-1 / 3628800)))))
    odd = (turns & 1) == 1
    cos = jnp.where(odd, s, c)
    sin = jnp.where(odd, c, s)
    cos = jnp.where(((turns + 1) & 2) == 2, -cos, cos)
    sin = jnp.where((turns & 2) == 2, -sin, sin)
    return cos, sin


def kernel(
    weights, mats, vertex, window, table, delta,
    slab, low, which, turn_cos, turn_sin, fine_cos, fine_sin, coarse_plus, coarse_minus, pair,
    partial, landed, gathered, wide, source, scaled,
    slab_sem, send_one, recv_one, send_two, recv_two,
):
    blk_count, walk_count, sub_count = (lax.axis_size(a) for a in ("blk", "walk", "sub"))
    b, w, s = (lax.axis_index(a) for a in ("blk", "walk", "sub"))
    near = walk_count * sub_count
    place = w * sub_count + s
    own_rows, depth = slab.shape
    rows = window.shape[0]
    share = rows // near
    columns = partial.shape[2]
    transfers = table.shape[0]
    rows_own = share // blk_count
    chunk = chunk_blocks * column_block
    chunks = columns // chunk
    start = pl.multiple_of(s * depth, lanes)
    fetch = pltpu.make_async_copy(mats.at[0, :, pl.ds(start, depth)], slab, slab_sem)
    fetch.start()

    def near_id(distance):
        peer = lax.rem(place + distance, near)
        return {"walk": peer // sub_count, "sub": lax.rem(peer, sub_count)}

    def far_id(distance):
        return {"blk": lax.rem(b + distance, blk_count)}

    def span_of(c):
        return pl.ds(pl.multiple_of(c * chunk, chunk), chunk)

    def near_copy(c, d):
        return pltpu.make_async_remote_copy(
            src_ref=partial.at[lax.rem(place + d, near), :, span_of(c)],
            dst_ref=landed.at[d - 1, :, span_of(c)],
            send_sem=send_one.at[c, d - 1],
            recv_sem=recv_one.at[c, d - 1],
            device_id=near_id(d),
            device_id_type=pl.DeviceIdType.MESH,
        )

    def far_copy(c, d):
        return pltpu.make_async_remote_copy(
            src_ref=gathered.at[0, :, span_of(c)],
            dst_ref=gathered.at[d, :, span_of(c)],
            send_sem=send_two.at[c, d - 1],
            recv_sem=recv_two.at[c, d - 1],
            device_id=far_id(d),
            device_id_type=pl.DeviceIdType.MESH,
        )

    barrier = pltpu.get_barrier_semaphore()
    for d in range(1, near):
        pl.semaphore_signal(barrier, inc=1, device_id=near_id(d), device_id_type=pl.DeviceIdType.MESH)
    for d in range(1, blk_count):
        pl.semaphore_signal(barrier, inc=1, device_id=far_id(d), device_id_type=pl.DeviceIdType.MESH)

    def row_of(count):
        return lax.broadcasted_iota(jnp.int32, (count, depth), 0)

    def phases(factor, verts):
        return cos_sin((factor * verts) & (half_period - 1))

    verts = vertex[:, pl.ds(start, depth)]
    own = vertex[:, pl.ds(pl.multiple_of(w * own_rows, lanes), own_rows)]
    cos, sin = phases(window[...] * 2, own)
    left = (cos + sin).astype(jnp.bfloat16)
    cos, sin = phases(row_of(coarse_plus.shape[0]) * (2 * column_block) + (column_block - 1), verts)
    coarse_plus[...] = cos + sin
    coarse_minus[...] = cos - sin
    steps = turn_cos.shape[0]
    cos, sin = phases(row_of(steps) * (2 * sublanes), verts)
    turn_cos[...] = cos
    turn_sin[...] = sin
    cos, sin = phases(row_of(sublanes) * 2 + 1, verts)
    for h in range(steps):
        ch, sh = turn_cos[h:h + 1, :], turn_sin[h:h + 1, :]
        fine_cos[h * sublanes:(h + 1) * sublanes, :] = ch * cos - sh * sin
        fine_sin[h * sublanes:(h + 1) * sublanes, :] = sh * cos + ch * sin

    fetch.wait()
    inner = jnp.dot(left, slab[...], preferred_element_type=jnp.float32)
    high = inner.astype(jnp.bfloat16)
    pair[0:rows, :] = high
    pair[rows:2 * rows, :] = (inner - high.astype(jnp.float32)).astype(jnp.bfloat16)

    pl.semaphore_wait(barrier, near - 1 + blk_count - 1)

    @pl.loop(0, chunks)
    def _(c):
        for part in range(chunk_blocks):
            block = c * chunk_blocks + part
            a_plus = coarse_plus[pl.ds(block, 1), :]
            a_minus = coarse_minus[pl.ds(block, 1), :]
            below, above = [], []
            for g in range(lanes // 16):
                p = a_plus * fine_cos[g * 16:(g + 1) * 16, :]
                q = a_minus * fine_sin[g * 16:(g + 1) * 16, :]
                below.append((p - q).astype(jnp.bfloat16))
                above.append((p + q).astype(jnp.bfloat16))
            both = lax.dot_general(
                pair[...], jnp.concatenate(below + above, axis=0), (((1,), (1,)), ((), ())),
                preferred_element_type=jnp.float32,
            )
            total = both[0:rows] + both[rows:2 * rows]
            here = pl.ds(pl.multiple_of(block * column_block, column_block), column_block)
            for q in range(near):
                partial[q, :, here] = total[q * share:(q + 1) * share]
        for d in range(1, near):
            near_copy(c, d).start()

    index = table[...]
    which[...] = index >> 7
    low[...] = (index & (lanes - 1)) ^ jnp.where((index & lanes) == 0, lanes - 1, 0)
    delta[...] = jnp.zeros_like(delta)

    @pl.loop(0, chunks)
    def _(c):
        here = span_of(c)
        total = partial[place, :, here]
        for d in range(1, near):
            near_copy(c, d).wait_recv()
            total = total + landed[d - 1, :, here]
        gathered[0, :, here] = total.astype(jnp.bfloat16)
        for d in range(1, blk_count):
            far_copy(c, d).start()

    back = lanes - 1 - lax.broadcasted_iota(jnp.int32, (sublanes, lanes), 1)

    def walker(d):
        wide[...] = gathered[d].astype(jnp.float32)
        weight = weights[lax.rem(b + blk_count - d, blk_count)] / weights.shape[0]
        for r in range(rows_own):
            for step in range(RSTEPS):
                row = lax.rem(b + RSTEPS * blk_count - step, blk_count) * rows_own + r
                line = wide[pl.ds(row, 1), :]
                source[step * TQ:(step + 1) * TQ, :] = jnp.broadcast_to(line, (TQ, columns))
                if step == 0:
                    tall = jnp.broadcast_to(line * weight, (sublanes, columns))
                    for k in range(columns // lanes):
                        piece = tall[:, k * lanes:(k + 1) * lanes]
                        if k % 2 == 0:
                            piece = jnp.take_along_axis(piece, back, axis=1, mode="promise_in_bounds")
                        scaled[:, k * lanes:(k + 1) * lanes] = piece

            @pl.loop(0, columns // (lanes * group_blocks))
            def _(group):
                for half in range(transfers // sublanes):
                    span = slice(half * sublanes, (half + 1) * sublanes)
                    heres = [
                        pl.ds(pl.multiple_of((group * group_blocks + i) * lanes, lanes), lanes)
                        for i in range(group_blocks)
                    ]
                    lows = [low[span, here] for here in heres]
                    blocks = [which[span, here] for here in heres]
                    picked = [jnp.zeros((sublanes, lanes), jnp.float32) for _ in heres]
                    for k in range(columns // lanes):
                        held = source[span, k * lanes:(k + 1) * lanes]
                        for i in range(group_blocks):
                            found = jnp.take_along_axis(held, lows[i], axis=1, mode="promise_in_bounds")
                            picked[i] = jnp.where(blocks[i] == k, found, picked[i])
                    for i, here in enumerate(heres):
                        delta[r, span, here] += picked[i] * scaled[:, here]

    walker(0)

    @pl.loop(1, blk_count)
    def _(d):
        for c in range(chunks):
            far_copy(c, d).wait_recv()
        walker(d)

    @pl.loop(0, chunks)
    def _(c):
        for d in range(1, near):
            near_copy(c, d).wait_send()
        for d in range(1, blk_count):
            far_copy(c, d).wait_send()


def local(walker_mats, vertex, weights, transfer_table, g4_old):
    blk_count, walk_count, sub_count = (lax.axis_size(a) for a in ("blk", "walk", "sub"))
    near = walk_count * sub_count
    rows_own, transfers, columns = g4_old.shape
    own_rows, vertices = walker_mats.shape[1:]
    depth = vertices // sub_count
    share = blk_count * rows_own
    rows = near * share
    chunks = columns // (column_block * chunk_blocks)
    coarse = -(-(columns // column_block) // sublanes) * sublanes
    p = np.arange(rows)
    inner, blk_part, near_part = p % rows_own, p // rows_own % blk_count, p // share
    window = jnp.asarray(((blk_part * near + near_part) * rows_own + inner)[:, None], jnp.int32)
    vmem = pl.BlockSpec(memory_space=pltpu.VMEM)
    delta = pl.pallas_call(
        kernel,
        out_shape=jax.ShapeDtypeStruct(g4_old.shape, jnp.float32),
        in_specs=[pl.BlockSpec(memory_space=pltpu.SMEM), pl.BlockSpec(memory_space=pl.ANY), vmem, vmem, vmem],
        out_specs=vmem,
        scratch_shapes=[
            pltpu.VMEM((own_rows, depth), jnp.bfloat16),
            pltpu.VMEM((transfers, columns), jnp.int32),
            pltpu.VMEM((transfers, columns), jnp.int32),
            pltpu.VMEM((lanes // sublanes, depth), jnp.float32),
            pltpu.VMEM((lanes // sublanes, depth), jnp.float32),
            pltpu.VMEM((lanes, depth), jnp.float32),
            pltpu.VMEM((lanes, depth), jnp.float32),
            pltpu.VMEM((coarse, depth), jnp.float32),
            pltpu.VMEM((coarse, depth), jnp.float32),
            pltpu.VMEM((2 * rows, depth), jnp.bfloat16),
            pltpu.VMEM((near, share, columns), jnp.float32),
            pltpu.VMEM((near - 1, share, columns), jnp.float32),
            pltpu.VMEM((blk_count, share, columns), jnp.bfloat16),
            pltpu.VMEM((share, columns), jnp.float32),
            pltpu.VMEM((transfers, columns), jnp.float32),
            pltpu.VMEM((sublanes, columns), jnp.float32),
            pltpu.SemaphoreType.DMA,
            pltpu.SemaphoreType.DMA((chunks, near - 1)),
            pltpu.SemaphoreType.DMA((chunks, near - 1)),
            pltpu.SemaphoreType.DMA((chunks, blk_count - 1)),
            pltpu.SemaphoreType.DMA((chunks, blk_count - 1)),
        ],
        compiler_params=pltpu.CompilerParams(collective_id=0, has_side_effects=True),
        name="panels",
    )(weights, walker_mats, vertex, window, transfer_table)
    return g4_old + delta


def solution(mesh):
    in_specs = (
        P(("grp", "blk"), "walk", None),
        P(("grp", "blk"), None),
        P("grp"),
        P(),
        P(("grp", "blk", "walk", "sub"), None, None),
    )
    out_specs = P(("grp", "blk", "walk", "sub"), None, None)
    return jax.shard_map(local, mesh=mesh, in_specs=in_specs, out_specs=out_specs, check_vma=False)
```

```python
import math

import jax
import jax.numpy as jnp
import numpy as np
from jax import lax
from jax.experimental import pallas as pl
from jax.experimental.pallas import tpu as pltpu
from jax.sharding import PartitionSpec as P

TQ = 4
RSTEPS = 4

half_period = 16384
lanes = 128
sublanes = 8
column_block = 256
chunk_blocks = 2


def cos_sin(residue):
    turns = (residue + half_period // 8) >> 12
    x = (residue - (turns << 12)).astype(jnp.float32) * (2.0 * math.pi / half_period)
    y = x * x
    s = x + x * y * (-1 / 6 + y * (1 / 120 + y * (-1 / 5040 + y * (1 / 362880))))
    c = 1.0 + y * (-0.5 + y * (1 / 24 + y * (-1 / 720 + y * (1 / 40320 + y * (-1 / 3628800)))))
    odd = (turns & 1) == 1
    cos = jnp.where(odd, s, c)
    sin = jnp.where(odd, c, s)
    cos = jnp.where(((turns + 1) & 2) == 2, -cos, cos)
    sin = jnp.where((turns & 2) == 2, -sin, sin)
    return cos, sin


def kernel(
    weights, mats, vertex, window, table, old, panels,
    slab, base, low, which, turn_cos, turn_sin, fine_cos, fine_sin, coarse_plus, coarse_minus, pair,
    partial, landed, gathered, wide, source, scaled,
    slab_sem, table_sem, base_sem, send_one, recv_one, send_two, recv_two,
):
    blk_count, walk_count, sub_count = (lax.axis_size(a) for a in ("blk", "walk", "sub"))
    b, w, s = (lax.axis_index(a) for a in ("blk", "walk", "sub"))
    near = walk_count * sub_count
    place = w * sub_count + s
    own_rows, depth = slab.shape
    rows = window.shape[0]
    share = rows // near
    columns = partial.shape[2]
    transfers = low.shape[0]
    rows_own = share // blk_count
    chunk = chunk_blocks * column_block
    chunks = columns // chunk
    start = pl.multiple_of(s * depth, lanes)
    fetch = pltpu.make_async_copy(mats.at[0, :, pl.ds(start, depth)], slab, slab_sem)
    fetch.start()
    fetch_table = pltpu.make_async_copy(table, low, table_sem)
    fetch_table.start()
    fetch_base = pltpu.make_async_copy(old, base, base_sem)
    fetch_base.start()

    def near_id(distance):
        peer = lax.rem(place + distance, near)
        return {"walk": peer // sub_count, "sub": lax.rem(peer, sub_count)}

    def far_id(distance):
        return {"blk": lax.rem(b + distance, blk_count)}

    def span_of(c):
        return pl.ds(pl.multiple_of(c * chunk, chunk), chunk)

    def near_copy(c, d):
        return pltpu.make_async_remote_copy(
            src_ref=partial.at[lax.rem(place + d, near), :, span_of(c)],
            dst_ref=landed.at[d - 1, :, span_of(c)],
            send_sem=send_one.at[c, d - 1],
            recv_sem=recv_one.at[c, d - 1],
            device_id=near_id(d),
            device_id_type=pl.DeviceIdType.MESH,
        )

    def far_copy(c, d):
        return pltpu.make_async_remote_copy(
            src_ref=gathered.at[0, :, span_of(c)],
            dst_ref=gathered.at[d, :, span_of(c)],
            send_sem=send_two.at[c, d - 1],
            recv_sem=recv_two.at[c, d - 1],
            device_id=far_id(d),
            device_id_type=pl.DeviceIdType.MESH,
        )

    barrier = pltpu.get_barrier_semaphore()
    for d in range(1, near):
        pl.semaphore_signal(barrier, inc=1, device_id=near_id(d), device_id_type=pl.DeviceIdType.MESH)
    for d in range(1, blk_count):
        pl.semaphore_signal(barrier, inc=1, device_id=far_id(d), device_id_type=pl.DeviceIdType.MESH)

    def row_of(count):
        return lax.broadcasted_iota(jnp.int32, (count, depth), 0)

    def phases(factor, verts):
        return cos_sin((factor * verts) & (half_period - 1))

    verts = vertex[:, pl.ds(start, depth)]
    own = vertex[:, pl.ds(pl.multiple_of(w * own_rows, lanes), own_rows)]
    cos, sin = phases(window[...] * 2, own)
    left = (cos + sin).astype(jnp.bfloat16)
    cos, sin = phases(row_of(coarse_plus.shape[0]) * (2 * column_block) + (column_block - 1), verts)
    coarse_plus[...] = cos + sin
    coarse_minus[...] = cos - sin
    steps = turn_cos.shape[0]
    cos, sin = phases(row_of(steps) * (2 * sublanes), verts)
    turn_cos[...] = cos
    turn_sin[...] = sin
    cos, sin = phases(row_of(sublanes) * 2 + 1, verts)

    for h in range(steps):
        ch, sh = turn_cos[h:h + 1, :], turn_sin[h:h + 1, :]
        fine_cos[h * sublanes:(h + 1) * sublanes, :] = ch * cos - sh * sin
        fine_sin[h * sublanes:(h + 1) * sublanes, :] = sh * cos + ch * sin

    fetch.wait()
    inner = jnp.dot(left, slab[...], preferred_element_type=jnp.float32)
    high = inner.astype(jnp.bfloat16)
    pair[0:rows, :] = high
    pair[rows:2 * rows, :] = (inner - high.astype(jnp.float32)).astype(jnp.bfloat16)

    pl.semaphore_wait(barrier, near - 1 + blk_count - 1)

    @pl.loop(0, chunks)
    def _(c):
        @pl.loop(0, chunk_blocks)
        def _(part):
            block = c * chunk_blocks + part
            a_plus = coarse_plus[pl.ds(block, 1), :]
            a_minus = coarse_minus[pl.ds(block, 1), :]
            below, above = [], []
            for g in range(lanes // 16):
                p = a_plus * fine_cos[g * 16:(g + 1) * 16, :]
                q = a_minus * fine_sin[g * 16:(g + 1) * 16, :]
                below.append((p - q).astype(jnp.bfloat16))
                above.append((p + q).astype(jnp.bfloat16))
            both = lax.dot_general(
                pair[...], jnp.concatenate(below + above, axis=0), (((1,), (1,)), ((), ())),
                preferred_element_type=jnp.float32,
            )
            total = both[0:rows] + both[rows:2 * rows]
            here = pl.ds(pl.multiple_of(block * column_block, column_block), column_block)
            for q in range(near):
                partial[q, :, here] = total[q * share:(q + 1) * share]

        for d in range(1, near):
            near_copy(c, d).start()

    fetch_table.wait()
    index = low[...]
    which[...] = index >> 7
    low[...] = (index & (lanes - 1)) ^ jnp.where((index & lanes) == 0, lanes - 1, 0)
    fetch_base.wait()
    panels[...] = base[...]

    @pl.loop(0, chunks)
    def _(c):
        here = span_of(c)
        total = partial[place, :, here]
        for d in range(1, near):
            near_copy(c, d).wait_recv()
            total = total + landed[d - 1, :, here]
        gathered[0, :, here] = total.astype(jnp.bfloat16)
        for d in range(1, blk_count):
            far_copy(c, d).start()

    back = lanes - 1 - lax.broadcasted_iota(jnp.int32, (sublanes, lanes), 1)

    def walkers(first, count, group_blocks):
        for r in range(rows_own):
            for n in range(count):
                wide[...] = gathered[first + n].astype(jnp.float32)
                weight = weights[lax.rem(b + blk_count - first - n, blk_count)] / weights.shape[0]
                for step in range(RSTEPS):
                    row = lax.rem(b + RSTEPS * blk_count - step, blk_count) * rows_own + r
                    line = wide[pl.ds(row, 1), :]
                    source[n, step * TQ:(step + 1) * TQ, :] = jnp.broadcast_to(line, (TQ, columns))
                    if step == 0:
                        tall = jnp.broadcast_to(line * weight, (sublanes, columns))
                        for k in range(columns // lanes):
                            piece = tall[:, k * lanes:(k + 1) * lanes]
                            if k % 2 == 0:
                                piece = jnp.take_along_axis(piece, back, axis=1, mode="promise_in_bounds")
                            scaled[n, :, k * lanes:(k + 1) * lanes] = piece

            @pl.loop(0, columns // (lanes * group_blocks))
            def _(group):
                for i in range(group_blocks):
                    here = pl.ds(pl.multiple_of((group * group_blocks + i) * lanes, lanes), lanes)
                    for half in range(transfers // sublanes):
                        span = slice(half * sublanes, (half + 1) * sublanes)
                        index = low[span, here]
                        block = which[span, here]
                        picked = [jnp.zeros((sublanes, lanes), jnp.float32) for _ in range(count)]
                        for k in range(columns // lanes):
                            hit = block == k
                            for n in range(count):
                                found = jnp.take_along_axis(
                                    source[n, span, k * lanes:(k + 1) * lanes], index, axis=1,
                                    mode="promise_in_bounds",
                                )
                                picked[n] = jnp.where(hit, found, picked[n])
                        total = picked[0] * scaled[0, :, here]
                        for n in range(1, count):
                            total = total + picked[n] * scaled[n, :, here]
                        panels[r, span, here] += total

    walkers(0, 1, 4)
    batch = source.shape[0]

    @pl.loop(0, (blk_count - 1) // batch)
    def _(g):
        first = 1 + g * batch
        for n in range(batch):
            for c in range(chunks):
                far_copy(c, first + n).wait_recv()
        walkers(first, batch, 2)

    @pl.loop(0, chunks)
    def _(c):
        for d in range(1, near):
            near_copy(c, d).wait_send()
        for d in range(1, blk_count):
            far_copy(c, d).wait_send()


def local(walker_mats, vertex, weights, transfer_table, g4_old):
    blk_count, walk_count, sub_count = (lax.axis_size(a) for a in ("blk", "walk", "sub"))
    near = walk_count * sub_count
    rows_own, transfers, columns = g4_old.shape
    own_rows, vertices = walker_mats.shape[1:]
    depth = vertices // sub_count
    share = blk_count * rows_own
    rows = near * share
    chunks = columns // (column_block * chunk_blocks)
    batch = max(n for n in (1, 2, 3) if (blk_count - 1) % n == 0)
    coarse = -(-(columns // column_block) // sublanes) * sublanes
    p = np.arange(rows)
    inner, blk_part, near_part = p % rows_own, p // rows_own % blk_count, p // share
    window = jnp.asarray(((blk_part * near + near_part) * rows_own + inner)[:, None], jnp.int32)
    vmem = pl.BlockSpec(memory_space=pltpu.VMEM)
    return pl.pallas_call(
        kernel,
        out_shape=jax.ShapeDtypeStruct(g4_old.shape, jnp.float32),
        in_specs=[pl.BlockSpec(memory_space=pltpu.SMEM), pl.BlockSpec(memory_space=pl.ANY), vmem, vmem]
        + [pl.BlockSpec(memory_space=pl.ANY)] * 2,
        out_specs=vmem,
        scratch_shapes=[
            pltpu.VMEM((own_rows, depth), jnp.bfloat16),
            pltpu.VMEM(g4_old.shape, jnp.float32),
            pltpu.VMEM((transfers, columns), jnp.int32),
            pltpu.VMEM((transfers, columns), jnp.int32),
            pltpu.VMEM((lanes // sublanes, depth), jnp.float32),
            pltpu.VMEM((lanes // sublanes, depth), jnp.float32),
            pltpu.VMEM((lanes, depth), jnp.float32),
            pltpu.VMEM((lanes, depth), jnp.float32),
            pltpu.VMEM((coarse, depth), jnp.float32),
            pltpu.VMEM((coarse, depth), jnp.float32),
            pltpu.VMEM((2 * rows, depth), jnp.bfloat16),
            pltpu.VMEM((near, share, columns), jnp.float32),
            pltpu.VMEM((near - 1, share, columns), jnp.float32),
            pltpu.VMEM((blk_count, share, columns), jnp.bfloat16),
            pltpu.VMEM((share, columns), jnp.float32),
            pltpu.VMEM((batch, transfers, columns), jnp.float32),
            pltpu.VMEM((batch, sublanes, columns), jnp.float32),
            pltpu.SemaphoreType.DMA,
            pltpu.SemaphoreType.DMA,
            pltpu.SemaphoreType.DMA,
            pltpu.SemaphoreType.DMA((chunks, near - 1)),
            pltpu.SemaphoreType.DMA((chunks, near - 1)),
            pltpu.SemaphoreType.DMA((chunks, blk_count - 1)),
            pltpu.SemaphoreType.DMA((chunks, blk_count - 1)),
        ],
        compiler_params=pltpu.CompilerParams(collective_id=0, has_side_effects=True),
        name="panels",
    )(weights, walker_mats, vertex, window, transfer_table, g4_old)


def solution(mesh):
    in_specs = (
        P(("grp", "blk"), "walk", None),
        P(("grp", "blk"), None),
        P("grp"),
        P(),
        P(("grp", "blk", "walk", "sub"), None, None),
    )
    out_specs = P(("grp", "blk", "walk", "sub"), None, None)
    return jax.shard_map(local, mesh=mesh, in_specs=in_specs, out_specs=out_specs, check_vma=False)
```

```python
import math

import jax
import jax.numpy as jnp
import numpy as np
from jax import lax
from jax.experimental import pallas as pl
from jax.experimental.pallas import tpu as pltpu
from jax.sharding import PartitionSpec as P

TQ = 4
RSTEPS = 4

half_period = 16384
lanes = 128
sublanes = 8
column_block = 256
chunk_blocks = 2


def cos_sin(residue):
    turns = (residue + half_period // 8) >> 12
    x = (residue - (turns << 12)).astype(jnp.float32) * (2.0 * math.pi / half_period)
    y = x * x
    s = x + x * y * (-1 / 6 + y * (1 / 120 + y * (-1 / 5040 + y * (1 / 362880))))
    c = 1.0 + y * (-0.5 + y * (1 / 24 + y * (-1 / 720 + y * (1 / 40320 + y * (-1 / 3628800)))))
    odd = (turns & 1) == 1
    cos = jnp.where(odd, s, c)
    sin = jnp.where(odd, c, s)
    cos = jnp.where(((turns + 1) & 2) == 2, -cos, cos)
    sin = jnp.where((turns & 2) == 2, -sin, sin)
    return cos, sin


def kernel(
    weights, mats, vertex, window, table, old, panels,
    slab, base, low, which, turn_cos, turn_sin, fine_cos, fine_sin, coarse_plus, coarse_minus, pair,
    partial, landed, gathered, wide, source, scaled,
    slab_sem, table_sem, base_sem, send_one, recv_one, send_two, recv_two,
):
    blk_count, walk_count, sub_count = (lax.axis_size(a) for a in ("blk", "walk", "sub"))
    b, w, s = (lax.axis_index(a) for a in ("blk", "walk", "sub"))
    near = walk_count * sub_count
    place = w * sub_count + s
    own_rows, depth = slab.shape
    rows = window.shape[0]
    share = rows // near
    columns = partial.shape[2]
    transfers = low.shape[0]
    rows_own = share // blk_count
    chunk = chunk_blocks * column_block
    chunks = columns // chunk
    start = pl.multiple_of(s * depth, lanes)
    fetch = pltpu.make_async_copy(mats.at[0, :, pl.ds(start, depth)], slab, slab_sem)
    fetch.start()
    fetch_table = pltpu.make_async_copy(table, low, table_sem)
    fetch_table.start()
    fetch_base = pltpu.make_async_copy(old, base, base_sem)
    fetch_base.start()

    def near_id(distance):
        peer = lax.rem(place + distance, near)
        return {"walk": peer // sub_count, "sub": lax.rem(peer, sub_count)}

    def far_id(distance):
        return {"blk": lax.rem(b + distance, blk_count)}

    def span_of(c):
        return pl.ds(pl.multiple_of(c * chunk, chunk), chunk)

    def near_copy(c, d):
        return pltpu.make_async_remote_copy(
            src_ref=partial.at[lax.rem(place + d, near), :, span_of(c)],
            dst_ref=landed.at[d - 1, :, span_of(c)],
            send_sem=send_one.at[c, d - 1],
            recv_sem=recv_one.at[c, d - 1],
            device_id=near_id(d),
            device_id_type=pl.DeviceIdType.MESH,
        )

    def far_copy(c, d):
        return pltpu.make_async_remote_copy(
            src_ref=gathered.at[0, :, span_of(c)],
            dst_ref=gathered.at[d, :, span_of(c)],
            send_sem=send_two.at[c, d - 1],
            recv_sem=recv_two.at[c, d - 1],
            device_id=far_id(d),
            device_id_type=pl.DeviceIdType.MESH,
        )

    barrier = pltpu.get_barrier_semaphore()
    for d in range(1, near):
        pl.semaphore_signal(barrier, inc=1, device_id=near_id(d), device_id_type=pl.DeviceIdType.MESH)
    for d in range(1, blk_count):
        pl.semaphore_signal(barrier, inc=1, device_id=far_id(d), device_id_type=pl.DeviceIdType.MESH)

    def row_of(count):
        return lax.broadcasted_iota(jnp.int32, (count, depth), 0)

    def phases(factor, verts):
        return cos_sin((factor * verts) & (half_period - 1))

    verts = vertex[:, pl.ds(start, depth)]
    own = vertex[:, pl.ds(pl.multiple_of(w * own_rows, lanes), own_rows)]
    cos, sin = phases(window[...] * 2, own)
    left = (cos + sin).astype(jnp.bfloat16)
    cos, sin = phases(row_of(coarse_plus.shape[0]) * (2 * column_block) + (column_block - 1), verts)
    coarse_plus[...] = cos + sin
    coarse_minus[...] = cos - sin
    steps = turn_cos.shape[0]
    cos, sin = phases(row_of(steps) * (2 * sublanes), verts)
    turn_cos[...] = cos
    turn_sin[...] = sin
    cos, sin = phases(row_of(sublanes) * 2 + 1, verts)

    for h in range(steps):
        ch, sh = turn_cos[h:h + 1, :], turn_sin[h:h + 1, :]
        fine_cos[h * sublanes:(h + 1) * sublanes, :] = ch * cos - sh * sin
        fine_sin[h * sublanes:(h + 1) * sublanes, :] = sh * cos + ch * sin

    fetch.wait()
    inner = jnp.dot(left, slab[...], preferred_element_type=jnp.float32)
    high = inner.astype(jnp.bfloat16)
    pair[0:rows, :] = high
    pair[rows:2 * rows, :] = (inner - high.astype(jnp.float32)).astype(jnp.bfloat16)

    pl.semaphore_wait(barrier, near - 1 + blk_count - 1)

    @pl.loop(0, chunks)
    def _(c):
        @pl.loop(0, chunk_blocks)
        def _(part):
            block = c * chunk_blocks + part
            a_plus = coarse_plus[pl.ds(block, 1), :]
            a_minus = coarse_minus[pl.ds(block, 1), :]
            below, above = [], []
            for g in range(lanes // 16):
                p = a_plus * fine_cos[g * 16:(g + 1) * 16, :]
                q = a_minus * fine_sin[g * 16:(g + 1) * 16, :]
                below.append((p - q).astype(jnp.bfloat16))
                above.append((p + q).astype(jnp.bfloat16))
            both = lax.dot_general(
                pair[...], jnp.concatenate(below + above, axis=0), (((1,), (1,)), ((), ())),
                preferred_element_type=jnp.float32,
            )
            total = both[0:rows] + both[rows:2 * rows]
            here = pl.ds(pl.multiple_of(block * column_block, column_block), column_block)
            for q in range(near):
                partial[q, :, here] = total[q * share:(q + 1) * share]

        for d in range(1, near):
            near_copy(c, d).start()

    fetch_table.wait()
    index = low[...]
    which[...] = index >> 7
    low[...] = (index & (lanes - 1)) ^ jnp.where((index & lanes) == 0, lanes - 1, 0)
    fetch_base.wait()
    panels[...] = base[...]

    @pl.loop(0, chunks)
    def _(c):
        here = span_of(c)
        total = partial[place, :, here]
        for d in range(1, near):
            near_copy(c, d).wait_recv()
            total = total + landed[d - 1, :, here]
        gathered[0, :, here] = total.astype(jnp.bfloat16)
        for d in range(1, blk_count):
            far_copy(c, d).start()

    back = lanes - 1 - lax.broadcasted_iota(jnp.int32, (sublanes, lanes), 1)

    def walkers(first, count, group_blocks):
        for r in range(rows_own):
            for n in range(count):
                wide[...] = gathered[first + n].astype(jnp.float32)
                weight = weights[lax.rem(b + blk_count - first - n, blk_count)] / weights.shape[0]
                for step in range(RSTEPS):
                    row = lax.rem(b + RSTEPS * blk_count - step, blk_count) * rows_own + r
                    line = wide[pl.ds(row, 1), :]
                    source[n, step * TQ:(step + 1) * TQ, :] = jnp.broadcast_to(line, (TQ, columns))
                    if step == 0:
                        tall = jnp.broadcast_to(line * weight, (sublanes, columns))
                        for k in range(columns // lanes):
                            piece = tall[:, k * lanes:(k + 1) * lanes]
                            if k % 2 == 0:
                                piece = jnp.take_along_axis(piece, back, axis=1, mode="promise_in_bounds")
                            scaled[n, :, k * lanes:(k + 1) * lanes] = piece

            @pl.loop(0, columns // (lanes * group_blocks))
            def _(group):
                for i in range(group_blocks):
                    here = pl.ds(pl.multiple_of((group * group_blocks + i) * lanes, lanes), lanes)
                    for half in range(transfers // sublanes):
                        span = slice(half * sublanes, (half + 1) * sublanes)
                        index = low[span, here]
                        block = which[span, here]
                        picked = [jnp.zeros((sublanes, lanes), jnp.float32) for _ in range(count)]
                        for k in range(columns // lanes):
                            hit = block == k
                            for n in range(count):
                                found = jnp.take_along_axis(
                                    source[n, span, k * lanes:(k + 1) * lanes], index, axis=1,
                                    mode="promise_in_bounds",
                                )
                                picked[n] = jnp.where(hit, found, picked[n])
                        total = picked[0] * scaled[0, :, here]
                        for n in range(1, count):
                            total = total + picked[n] * scaled[n, :, here]
                        panels[r, span, here] += total

    walkers(0, 1, 4)

    @pl.loop(0, blk_count - 1)
    def _(i):
        origin = i + (i + blk_count - b) // blk_count
        d = lax.rem(b + blk_count - origin, blk_count)
        for c in range(chunks):
            far_copy(c, d).wait_recv()
        walkers(d, 1, 4)

    @pl.loop(0, chunks)
    def _(c):
        for d in range(1, near):
            near_copy(c, d).wait_send()
        for d in range(1, blk_count):
            far_copy(c, d).wait_send()


def local(walker_mats, vertex, weights, transfer_table, g4_old):
    blk_count, walk_count, sub_count = (lax.axis_size(a) for a in ("blk", "walk", "sub"))
    near = walk_count * sub_count
    rows_own, transfers, columns = g4_old.shape
    own_rows, vertices = walker_mats.shape[1:]
    depth = vertices // sub_count
    share = blk_count * rows_own
    rows = near * share
    chunks = columns // (column_block * chunk_blocks)
    coarse = -(-(columns // column_block) // sublanes) * sublanes
    p = np.arange(rows)
    inner, blk_part, near_part = p % rows_own, p // rows_own % blk_count, p // share
    window = jnp.asarray(((blk_part * near + near_part) * rows_own + inner)[:, None], jnp.int32)
    vmem = pl.BlockSpec(memory_space=pltpu.VMEM)
    return pl.pallas_call(
        kernel,
        out_shape=pltpu.VMEM(g4_old.shape, jnp.float32),
        in_specs=[pl.BlockSpec(memory_space=pltpu.SMEM), pl.BlockSpec(memory_space=pl.ANY), vmem, vmem]
        + [pl.BlockSpec(memory_space=pl.ANY)] * 2,
        out_specs=vmem,
        scratch_shapes=[
            pltpu.VMEM((own_rows, depth), jnp.bfloat16),
            pltpu.VMEM(g4_old.shape, jnp.float32),
            pltpu.VMEM((transfers, columns), jnp.int32),
            pltpu.VMEM((transfers, columns), jnp.int32),
            pltpu.VMEM((lanes // sublanes, depth), jnp.float32),
            pltpu.VMEM((lanes // sublanes, depth), jnp.float32),
            pltpu.VMEM((lanes, depth), jnp.float32),
            pltpu.VMEM((lanes, depth), jnp.float32),
            pltpu.VMEM((coarse, depth), jnp.float32),
            pltpu.VMEM((coarse, depth), jnp.float32),
            pltpu.VMEM((2 * rows, depth), jnp.bfloat16),
            pltpu.VMEM((near, share, columns), jnp.float32),
            pltpu.VMEM((near - 1, share, columns), jnp.float32),
            pltpu.VMEM((blk_count, share, columns), jnp.bfloat16),
            pltpu.VMEM((share, columns), jnp.float32),
            pltpu.VMEM((1, transfers, columns), jnp.float32),
            pltpu.VMEM((1, sublanes, columns), jnp.float32),
            pltpu.SemaphoreType.DMA,
            pltpu.SemaphoreType.DMA,
            pltpu.SemaphoreType.DMA,
            pltpu.SemaphoreType.DMA((chunks, near - 1)),
            pltpu.SemaphoreType.DMA((chunks, near - 1)),
            pltpu.SemaphoreType.DMA((chunks, blk_count - 1)),
            pltpu.SemaphoreType.DMA((chunks, blk_count - 1)),
        ],
        compiler_params=pltpu.CompilerParams(collective_id=0, has_side_effects=True),
        name="panels",
    )(weights, walker_mats, vertex, window, transfer_table, g4_old)


def solution(mesh):
    in_specs = (
        P(("grp", "blk"), "walk", None),
        P(("grp", "blk"), None),
        P("grp"),
        P(),
        P(("grp", "blk", "walk", "sub"), None, None),
    )
    out_specs = P(("grp", "blk", "walk", "sub"), None, None)
    return jax.shard_map(local, mesh=mesh, in_specs=in_specs, out_specs=out_specs, check_vma=False)
```

```python
import math

import jax
import jax.numpy as jnp
import numpy as np
from jax import lax
from jax.experimental import pallas as pl
from jax.experimental.pallas import tpu as pltpu
from jax.sharding import PartitionSpec as P

TQ = 4
RSTEPS = 4

half_period = 16384
lanes = 128
sublanes = 8
column_block = 256
chunk_blocks = 2


def cos_sin(residue):
    turns = (residue + half_period // 8) >> 12
    x = (residue - (turns << 12)).astype(jnp.float32) * (2.0 * math.pi / half_period)
    y = x * x
    s = x + x * y * (-1 / 6 + y * (1 / 120 + y * (-1 / 5040 + y * (1 / 362880))))
    c = 1.0 + y * (-0.5 + y * (1 / 24 + y * (-1 / 720 + y * (1 / 40320 + y * (-1 / 3628800)))))
    odd = (turns & 1) == 1
    cos = jnp.where(odd, s, c)
    sin = jnp.where(odd, c, s)
    cos = jnp.where(((turns + 1) & 2) == 2, -cos, cos)
    sin = jnp.where((turns & 2) == 2, -sin, sin)
    return cos, sin


def kernel(
    weights, mats, vertex, window, table, old, panels,
    slab, base, low, which, turn_cos, turn_sin, fine_cos, fine_sin, coarse_plus, coarse_minus, pair,
    partial, landed, gathered, wide, source, scaled,
    slab_sem, table_sem, base_sem, send_one, recv_one, send_two, recv_two,
):
    blk_count, walk_count, sub_count = (lax.axis_size(a) for a in ("blk", "walk", "sub"))
    b, w, s = (lax.axis_index(a) for a in ("blk", "walk", "sub"))
    near = walk_count * sub_count
    place = w * sub_count + s
    own_rows, depth = slab.shape
    rows = window.shape[0]
    share = rows // near
    columns = partial.shape[2]
    transfers = low.shape[0]
    rows_own = share // blk_count
    chunk = chunk_blocks * column_block
    chunks = columns // chunk
    start = pl.multiple_of(s * depth, lanes)
    fetch = pltpu.make_async_copy(mats.at[0, :, pl.ds(start, depth)], slab, slab_sem)
    fetch.start()
    fetch_table = pltpu.make_async_copy(table, low, table_sem)
    fetch_table.start()
    fetch_base = pltpu.make_async_copy(old, base, base_sem)
    fetch_base.start()

    def near_id(distance):
        peer = lax.rem(place + distance, near)
        return {"walk": peer // sub_count, "sub": lax.rem(peer, sub_count)}

    def far_id(distance):
        return {"blk": lax.rem(b + distance, blk_count)}

    def span_of(c):
        return pl.ds(pl.multiple_of(c * chunk, chunk), chunk)

    def near_copy(c, d):
        return pltpu.make_async_remote_copy(
            src_ref=partial.at[lax.rem(place + d, near), :, span_of(c)],
            dst_ref=landed.at[d - 1, :, span_of(c)],
            send_sem=send_one.at[c, d - 1],
            recv_sem=recv_one.at[c, d - 1],
            device_id=near_id(d),
            device_id_type=pl.DeviceIdType.MESH,
        )

    def far_copy(c, d):
        return pltpu.make_async_remote_copy(
            src_ref=gathered.at[0, :, span_of(c)],
            dst_ref=gathered.at[d, :, span_of(c)],
            send_sem=send_two.at[c, d - 1],
            recv_sem=recv_two.at[c, d - 1],
            device_id=far_id(d),
            device_id_type=pl.DeviceIdType.MESH,
        )

    barrier = pltpu.get_barrier_semaphore()
    for d in range(1, near):
        pl.semaphore_signal(barrier, inc=1, device_id=near_id(d), device_id_type=pl.DeviceIdType.MESH)
    for d in range(1, blk_count):
        pl.semaphore_signal(barrier, inc=1, device_id=far_id(d), device_id_type=pl.DeviceIdType.MESH)

    def row_of(count):
        return lax.broadcasted_iota(jnp.int32, (count, depth), 0)

    def phases(factor, verts):
        return cos_sin((factor * verts) & (half_period - 1))

    verts = vertex[:, pl.ds(start, depth)]
    own = vertex[:, pl.ds(pl.multiple_of(w * own_rows, lanes), own_rows)]
    cos, sin = phases(window[...] * 2, own)
    left = (cos + sin).astype(jnp.bfloat16)
    cos, sin = phases(row_of(coarse_plus.shape[0]) * (2 * column_block) + (column_block - 1), verts)
    coarse_plus[...] = cos + sin
    coarse_minus[...] = cos - sin
    steps = turn_cos.shape[0]
    cos, sin = phases(row_of(steps) * (2 * sublanes), verts)
    turn_cos[...] = cos
    turn_sin[...] = sin
    cos, sin = phases(row_of(sublanes) * 2 + 1, verts)

    fetch.wait()
    inner = jnp.dot(left, slab[...], preferred_element_type=jnp.float32)
    for h in range(steps):
        ch, sh = turn_cos[h:h + 1, :], turn_sin[h:h + 1, :]
        fine_cos[h * sublanes:(h + 1) * sublanes, :] = ch * cos - sh * sin
        fine_sin[h * sublanes:(h + 1) * sublanes, :] = sh * cos + ch * sin

    high = inner.astype(jnp.bfloat16)
    pair[0:rows, :] = high
    pair[rows:2 * rows, :] = (inner - high.astype(jnp.float32)).astype(jnp.bfloat16)

    pl.semaphore_wait(barrier, near - 1 + blk_count - 1)

    @pl.loop(0, chunks)
    def _(c):
        @pl.loop(0, chunk_blocks)
        def _(part):
            block = c * chunk_blocks + part
            a_plus = coarse_plus[pl.ds(block, 1), :]
            a_minus = coarse_minus[pl.ds(block, 1), :]
            both = jnp.zeros((2 * rows, column_block), jnp.float32)
            for k in range(depth // 256):
                tile = slice(k * 256, (k + 1) * 256)
                below, above = [], []
                for g in range(lanes // 16):
                    p = a_plus[:, tile] * fine_cos[g * 16:(g + 1) * 16, tile]
                    q = a_minus[:, tile] * fine_sin[g * 16:(g + 1) * 16, tile]
                    below.append((p - q).astype(jnp.bfloat16))
                    above.append((p + q).astype(jnp.bfloat16))
                both = both + lax.dot_general(
                    pair[:, tile], jnp.concatenate(below + above, axis=0), (((1,), (1,)), ((), ())),
                    preferred_element_type=jnp.float32,
                )
            total = both[0:rows] + both[rows:2 * rows]
            here = pl.ds(pl.multiple_of(block * column_block, column_block), column_block)
            for q in range(near):
                partial[q, :, here] = total[q * share:(q + 1) * share]

        for d in range(1, near):
            near_copy(c, d).start()

    fetch_table.wait()
    index = low[...]
    which[...] = index >> 7
    low[...] = (index & (lanes - 1)) ^ jnp.where((index & lanes) == 0, lanes - 1, 0)
    fetch_base.wait()
    panels[...] = base[...]

    @pl.loop(0, chunks)
    def _(c):
        here = span_of(c)
        total = partial[place, :, here]
        for d in range(1, near):
            near_copy(c, d).wait_recv()
            total = total + landed[d - 1, :, here]
        gathered[0, :, here] = total.astype(jnp.bfloat16)
        for d in range(1, blk_count):
            far_copy(c, d).start()

    back = lanes - 1 - lax.broadcasted_iota(jnp.int32, (sublanes, lanes), 1)

    def walkers(first, count, group_blocks):
        for r in range(rows_own):
            for n in range(count):
                wide[...] = gathered[first + n].astype(jnp.float32)
                weight = weights[lax.rem(b + blk_count - first - n, blk_count)] / weights.shape[0]
                for step in range(RSTEPS):
                    row = lax.rem(b + RSTEPS * blk_count - step, blk_count) * rows_own + r
                    line = wide[pl.ds(row, 1), :]
                    source[n, step * TQ:(step + 1) * TQ, :] = jnp.broadcast_to(line, (TQ, columns))
                    if step == 0:
                        tall = jnp.broadcast_to(line * weight, (sublanes, columns))
                        for k in range(columns // lanes):
                            piece = tall[:, k * lanes:(k + 1) * lanes]
                            if k % 2 == 0:
                                piece = jnp.take_along_axis(piece, back, axis=1, mode="promise_in_bounds")
                            scaled[n, :, k * lanes:(k + 1) * lanes] = piece

            @pl.loop(0, columns // (lanes * group_blocks))
            def _(group):
                for i in range(group_blocks):
                    here = pl.ds(pl.multiple_of((group * group_blocks + i) * lanes, lanes), lanes)
                    for half in range(transfers // sublanes):
                        span = slice(half * sublanes, (half + 1) * sublanes)
                        index = low[span, here]
                        block = which[span, here]
                        picked = [jnp.zeros((sublanes, lanes), jnp.float32) for _ in range(count)]
                        for k in range(columns // lanes):
                            hit = block == k
                            for n in range(count):
                                found = jnp.take_along_axis(
                                    source[n, span, k * lanes:(k + 1) * lanes], index, axis=1,
                                    mode="promise_in_bounds",
                                )
                                picked[n] = jnp.where(hit, found, picked[n])
                        total = picked[0] * scaled[0, :, here]
                        for n in range(1, count):
                            total = total + picked[n] * scaled[n, :, here]
                        panels[r, span, here] += total

    walkers(0, 1, 4)

    @pl.loop(0, blk_count - 1)
    def _(i):
        origin = i + (i + blk_count - b) // blk_count
        d = lax.rem(b + blk_count - origin, blk_count)
        for c in range(chunks):
            far_copy(c, d).wait_recv()
        walkers(d, 1, 4)

    @pl.loop(0, chunks)
    def _(c):
        for d in range(1, near):
            near_copy(c, d).wait_send()
        for d in range(1, blk_count):
            far_copy(c, d).wait_send()


def local(walker_mats, vertex, weights, transfer_table, g4_old):
    blk_count, walk_count, sub_count = (lax.axis_size(a) for a in ("blk", "walk", "sub"))
    near = walk_count * sub_count
    rows_own, transfers, columns = g4_old.shape
    own_rows, vertices = walker_mats.shape[1:]
    depth = vertices // sub_count
    share = blk_count * rows_own
    rows = near * share
    chunks = columns // (column_block * chunk_blocks)
    coarse = -(-(columns // column_block) // sublanes) * sublanes
    p = np.arange(rows)
    inner, blk_part, near_part = p % rows_own, p // rows_own % blk_count, p // share
    window = jnp.asarray(((blk_part * near + near_part) * rows_own + inner)[:, None], jnp.int32)
    vmem = pl.BlockSpec(memory_space=pltpu.VMEM)
    return pl.pallas_call(
        kernel,
        out_shape=pltpu.VMEM(g4_old.shape, jnp.float32),
        in_specs=[pl.BlockSpec(memory_space=pltpu.SMEM), pl.BlockSpec(memory_space=pl.ANY), vmem, vmem]
        + [pl.BlockSpec(memory_space=pl.ANY)] * 2,
        out_specs=vmem,
        scratch_shapes=[
            pltpu.VMEM((own_rows, depth), jnp.bfloat16),
            pltpu.VMEM(g4_old.shape, jnp.float32),
            pltpu.VMEM((transfers, columns), jnp.int32),
            pltpu.VMEM((transfers, columns), jnp.int32),
            pltpu.VMEM((lanes // sublanes, depth), jnp.float32),
            pltpu.VMEM((lanes // sublanes, depth), jnp.float32),
            pltpu.VMEM((lanes, depth), jnp.float32),
            pltpu.VMEM((lanes, depth), jnp.float32),
            pltpu.VMEM((coarse, depth), jnp.float32),
            pltpu.VMEM((coarse, depth), jnp.float32),
            pltpu.VMEM((2 * rows, depth), jnp.bfloat16),
            pltpu.VMEM((near, share, columns), jnp.float32),
            pltpu.VMEM((near - 1, share, columns), jnp.float32),
            pltpu.VMEM((blk_count, share, columns), jnp.bfloat16),
            pltpu.VMEM((share, columns), jnp.float32),
            pltpu.VMEM((1, transfers, columns), jnp.float32),
            pltpu.VMEM((1, sublanes, columns), jnp.float32),
            pltpu.SemaphoreType.DMA,
            pltpu.SemaphoreType.DMA,
            pltpu.SemaphoreType.DMA,
            pltpu.SemaphoreType.DMA((chunks, near - 1)),
            pltpu.SemaphoreType.DMA((chunks, near - 1)),
            pltpu.SemaphoreType.DMA((chunks, blk_count - 1)),
            pltpu.SemaphoreType.DMA((chunks, blk_count - 1)),
        ],
        compiler_params=pltpu.CompilerParams(collective_id=0, has_side_effects=True),
        name="panels",
    )(weights, walker_mats, vertex, window, transfer_table, g4_old)


def solution(mesh):
    in_specs = (
        P(("grp", "blk"), "walk", None),
        P(("grp", "blk"), None),
        P("grp"),
        P(),
        P(("grp", "blk", "walk", "sub"), None, None),
    )
    out_specs = P(("grp", "blk", "walk", "sub"), None, None)
    return jax.shard_map(local, mesh=mesh, in_specs=in_specs, out_specs=out_specs, check_vma=False)
```
